32 devices in a mesh: groups: 2 (over y), rec: 4 (over z), attr: 4 (over x, core).
Axes of the slice: x: 2, y: 2, z: 4, core: 2. Of those that a mesh axis runs over, the one named last changes fastest.
Arguments:
- cells: bfloat16 [64, 49152], P(('groups', 'rec'), 'attr'), parts along dimension 0, may hold values from -1000 to 1000
- cotangent: bfloat16 [64, 49152], P(('groups', 'rec'), 'attr'), parts along dimension 0, may hold values from -6 to 6
- qkv_attr: bfloat16 [192, 576], replicated, may hold values from -8 to 8
- out_attr: bfloat16 [192, 192], replicated, may hold values from -0.4375 to 0.4375
- qkv_samp: bfloat16 [192, 576], replicated, may hold values from -8 to 8
- out_samp: bfloat16 [192, 192], replicated, may hold values from -0.4375 to 0.4375
- up_weight: bfloat16 [192, 768], replicated, may hold values from -0.4375 to 0.4375
- down_weight: bfloat16 [768, 192], replicated, may hold values from -0.21875 to 0.21875
- train_split: int32 [64], P('groups'), parts along dimension 0, may hold values from 0 to 1, as said below
Outputs:
- grad_cells: bfloat16 [64, 49152], P(('groups', 'rec'), 'attr'), parts along dimension 0
- grad_qkv_attr: float32 [384, 576], P('groups'), parts along dimension 0
- grad_out_attr: float32 [384, 192], P('groups'), parts along dimension 0
- grad_qkv_samp: float32 [384, 576], P('groups'), parts along dimension 0
- grad_out_samp: float32 [384, 192], P('groups'), parts along dimension 0
- grad_up: float32 [384, 768], P('groups'), parts along dimension 0
- grad_down: float32 [1536, 192], P('groups'), parts along dimension 0
The draws below stay inside these ranges and needn't reach their ends.
There are 2 independent parts, one for each index of `groups`. The reference program is written for one: setup_inputs(seed, part) draws one part's arguments, and reference() takes and returns one part's arrays. A program takes and returns all parts, laid end to end along the dimension named above; an argument that names none is the same for every part. Nothing has to cross between parts.
Inputs may be any that keep to these rules, and one draw needn't show every extreme that they name: `train_split`: every table window has at least one training record.
All inputs are finite; a program needn't handle non-finite values.
Results may differ from the reference program's by a relative error of at most 0.018.
The reference program's roundings to bfloat16 on the way count: a program that leaves them out, or rounds other values in their place, can miss the bound.
Values may be sent and summed in bfloat16 or wider, within the bound.
A program may use at most 64 MiB of HBM per device.

```python
import math
import jax
import jax.numpy as jnp
from jax import lax

E = 192
HEADS = 6
FF = 768
RECORDS = 32
ATTRS = 256


def qkv_draw(key):
    base_key = jax.random.fold_in(key, 0)
    matrix = jax.random.normal(base_key, (E, 3 * E), jnp.float32) / math.sqrt(E)
    return matrix


def draw_qkv_attr(key, part):
    return qkv_draw(jax.random.fold_in(key, 11)).astype(jnp.bfloat16)


def draw_qkv_samp(key, part):
    return qkv_draw(jax.random.fold_in(key, 12)).astype(jnp.bfloat16)


def draw_cells(key, part):
    keys_all = jax.random.split(jax.random.fold_in(key, 13), 3)
    cell_scale = jnp.exp(jax.random.uniform(keys_all[1], (RECORDS, ATTRS, 1), jnp.float32, 0.0, math.log(10.0)))
    feature_scale = jnp.exp(jax.random.uniform(keys_all[2], (1, 1, E), jnp.float32, 0.0, math.log(10.0)))
    base = jax.random.normal(keys_all[0], (RECORDS, ATTRS, E), jnp.float32)
    return (base * cell_scale * feature_scale).reshape(RECORDS, ATTRS * E).astype(jnp.bfloat16)


def draw_train_split(key, part):
    first_key, second_key = jax.random.split(jax.random.fold_in(key, 14))
    coins = jax.random.randint(first_key, (RECORDS,), 0, 2)
    chosen = jax.random.randint(second_key, (), 0, RECORDS)
    return jnp.where(jnp.arange(RECORDS) == chosen, 1, coins).astype(jnp.int32)


def steps_of(stream_key, extent, cuts, low, high):
    factor_of, own = 1.0, jax.random.fold_in(stream_key, 6)
    for position, shards_of in cuts:
        steps = jnp.exp(jax.random.uniform(jax.random.fold_in(own, position), (shards_of,), jnp.float32, low / len(cuts), high / len(cuts)))
        factor_of = factor_of * jnp.repeat(steps, extent[position] // shards_of).reshape([-1 if axis == position else 1 for axis in range(len(extent))])
    return factor_of


def bell_draw(own_key, dims, deviation, limit, pieces=(), dtype=jnp.bfloat16):
    level = steps_of(own_key, dims, pieces, -0.22, 0.18) if pieces else 1.0
    result = jax.random.normal(own_key, dims, jnp.float32) * deviation * level
    return jnp.minimum(jnp.maximum(result, -limit), limit).astype(dtype)


def setup_inputs(seed: int = 0, part: int = 0) -> dict:
    seeds = jax.random.split(jax.random.key(seed), 10)
    own_keys = jax.random.split(jax.random.fold_in(seeds[9], part), 10)
    cells = draw_cells(jax.random.fold_in(jax.random.fold_in(seeds[9], part), 71), part)
    cotangent = bell_draw(own_keys[1], (RECORDS, ATTRS * E), 1.0, 6.0, ((0, 4), (1, 4)))
    qkv_attr = draw_qkv_attr(jax.random.fold_in(seeds[9], 71), part)
    out_attr = bell_draw(seeds[3], (E, E), E ** -0.5, 0.4375)
    qkv_samp = draw_qkv_samp(jax.random.fold_in(seeds[9], 71), part)
    out_samp = bell_draw(seeds[5], (E, E), E ** -0.5, 0.4375)
    up_weight = bell_draw(seeds[6], (E, FF), E ** -0.5, 0.4375)
    down_weight = bell_draw(seeds[7], (FF, E), FF ** -0.5, 0.21875)
    train_split = draw_train_split(jax.random.fold_in(jax.random.fold_in(seeds[9], part), 71), part)
    return {"cells": cells, "cotangent": cotangent, "qkv_attr": qkv_attr, "out_attr": out_attr, "qkv_samp": qkv_samp, "out_samp": out_samp, "up_weight": up_weight, "down_weight": down_weight, "train_split": train_split}


def product(form, left, right):
    return jnp.einsum(form, left.astype(jnp.float32), right.astype(jnp.float32))

def layer_norm(values):
    center = values - lax.optimization_barrier(jnp.mean(values, axis=-1, keepdims=True))
    spread = lax.optimization_barrier(jnp.mean(center * center, axis=-1, keepdims=True))
    return center * lax.rsqrt(spread + 1e-05)

def attend(cells_in, qkv_weight, out_weight, allowed):
    groups, length, width = cells_in.shape
    head_dim = width // HEADS
    as_float = cells_in.astype(jnp.float32)
    normed = layer_norm(as_float).astype(jnp.bfloat16)
    project = product('gle,ef->glf', normed, qkv_weight).astype(jnp.bfloat16)
    project = project.reshape(groups, length, 3, HEADS, head_dim)
    scores = product('gqhd,gkhd->ghqk', project[:, :, 0], project[:, :, 1]) * (1.0 / math.sqrt(head_dim))
    if allowed is not None:
        scores = jnp.where(allowed[None, None, None, :] > 0, scores, -1e+30)
    top_score = lax.stop_gradient(lax.optimization_barrier(jnp.max(scores, axis=-1, keepdims=True)))
    expo = jnp.exp(scores - top_score)
    probs = (expo / lax.optimization_barrier(jnp.sum(expo, axis=-1, keepdims=True))).astype(jnp.bfloat16)
    mixed = product('ghqk,gkhd->gqhd', probs, project[:, :, 2]).astype(jnp.bfloat16)
    mixed = mixed.reshape(groups, length, width)
    return (as_float + product('gle,ef->glf', mixed, out_weight)).astype(jnp.bfloat16)

def feed_forward(block, up_weight, down_weight):
    flat = block.reshape(-1, E)
    as_float = flat.astype(jnp.float32)
    normed = layer_norm(as_float).astype(jnp.bfloat16)
    hidden = jax.nn.gelu(product('re,ef->rf', normed, up_weight), approximate=False).astype(jnp.bfloat16)
    return (as_float + product('rf,fe->re', hidden, down_weight)).astype(jnp.bfloat16).reshape(block.shape)

def reference(cells, cotangent, qkv_attr, out_attr, qkv_samp, out_samp, up_weight, down_weight, train_split):
    rec_block = math.gcd(RECORDS, 8)
    attr_block = math.gcd(ATTRS, 8)

    def forward(table_flat, qa_weight, oa_weight, qs_weight, os_weight, first_weight, second_weight):
        table = table_flat.reshape(RECORDS // rec_block, rec_block, ATTRS, E)

        def attr_step(piece):
            return attend(piece, qa_weight, oa_weight, None)
        first = lax.map(jax.checkpoint(attr_step), table).reshape(RECORDS, ATTRS, E)
        turned = jnp.swapaxes(first, 0, 1).reshape(ATTRS // attr_block, attr_block, RECORDS, E)

        def samp_step(piece):
            return attend(piece, qs_weight, os_weight, train_split)
        second = lax.map(jax.checkpoint(samp_step), turned).reshape(ATTRS, RECORDS, E)
        second = jnp.swapaxes(second, 0, 1)
        return feed_forward(second, first_weight, second_weight).reshape(RECORDS, ATTRS * E)
    weights = (qkv_attr, out_attr, qkv_samp, out_samp, up_weight, down_weight)
    weights = tuple((matrix.astype(jnp.float32) for matrix in weights))
    output_cells, puller = jax.vjp(forward, cells, *weights)
    grads = puller(cotangent)
    factor = 1.0 / math.sqrt(RECORDS * ATTRS)
    return (grads[0], grads[1] * factor, grads[2] * factor, grads[3] * factor, grads[4] * factor, grads[5] * factor, grads[6] * factor)
```

```python
import functools
import math

import jax
import jax.numpy as jnp
import numpy as np
from jax import lax
from jax.experimental import pallas as pl
from jax.experimental.pallas import tpu as pltpu
from jax.sharding import PartitionSpec as P

E = 192
HEADS = 6
HD = E // HEADS
SCALE = 1.0 / math.sqrt(HD)
BLOCKS = 16
F32 = jnp.float32
BF16 = jnp.bfloat16
MESH = pl.DeviceIdType.MESH
NN = (((1,), (0,)), ((), ()))
NT = (((1,), (1,)), ((), ()))
TN = (((0,), (0,)), ((), ()))
VMEM = pl.BlockSpec(memory_space=pltpu.VMEM)


def dot(a, b, form=NN):
    return lax.dot_general(a, b, form, preferred_element_type=F32)


def place(sizes, order):
    index = np.arange(math.prod(sizes)).reshape(sizes).transpose(order).reshape(-1)
    there = np.empty_like(index)
    there[index] = np.arange(index.size)
    return jnp.asarray(there.astype(np.int32)[None, :])


def moved(where_ref, x):
    n = x.shape[0]
    hot = lax.broadcasted_iota(jnp.int32, (n, n), 0) == where_ref[...]
    return dot(jnp.where(hot, 1.0, 0.0).astype(BF16), x)


def norm(x):
    center = x - jnp.mean(x, axis=-1, keepdims=True)
    scale = lax.rsqrt(jnp.mean(center * center, axis=-1, keepdims=True) + 1e-05)
    return center * scale, scale


def norm_back(hat, scale, grad):
    return scale * (
        grad
        - jnp.mean(grad, axis=-1, keepdims=True)
        - hat * jnp.mean(grad * hat, axis=-1, keepdims=True)
    )


def head_mask(h):
    lane = lax.broadcasted_iota(jnp.int32, (1, E), 1)
    return jnp.where((lane >= h * HD) & (lane < (h + 1) * HD), 1.0, 0.0).astype(F32)


def attend(x_ref, qkv, out, qkv_s, p_s, acc, n, size, bias):
    normed = norm(x_ref[...].astype(F32))[0].astype(BF16)
    for t in range(3):
        qkv_s[t] = dot(normed, qkv[:, t * E:(t + 1) * E]).astype(BF16)
    acc[0] = jnp.zeros(acc.shape[1:], F32)

    def head(h, _):
        mask = head_mask(h)
        for b in range(n):
            rows = pl.ds(b * size, size)
            s = dot(qkv_s[0, rows] * mask.astype(BF16), qkv_s[1, rows], NT) * SCALE
            if bias is not None:
                s = jnp.where(bias[...] > 0, s, -1e30)
            e = jnp.exp(s - jnp.max(s, axis=-1, keepdims=True))
            p = e * (1.0 / jnp.sum(e, axis=-1, keepdims=True))
            p_s[b, h] = p
            acc[0, rows] += dot(p.astype(BF16), qkv_s[2, rows]) * mask
        return 0

    lax.fori_loop(0, HEADS, head, 0)
    mixed = acc[0].astype(BF16)
    return normed, mixed, (x_ref[...].astype(F32) + dot(mixed, out)).astype(BF16)


def attend_back(x, g, mixed, qkv, out, qkv_s, p_s, acc, dm_s, grads, first, n, size):
    dm_s[...] = dot(g, out, NT).astype(BF16)
    grads[first + 3] = dot(mixed, g, TN).astype(BF16)
    acc[...] = jnp.zeros(acc.shape, F32)

    def head(h, _):
        mask = head_mask(h)
        for b in range(n):
            rows = pl.ds(b * size, size)
            dm = dm_s[rows] * mask.astype(BF16)
            p = p_s[b, h]
            dp = dot(dm, qkv_s[2, rows], NT).astype(BF16).astype(F32)
            ds = (p * (dp - jnp.sum(dp * p, axis=-1, keepdims=True)) * SCALE).astype(BF16)
            acc[0, rows] += dot(ds, qkv_s[1, rows]) * mask
            acc[1, rows] += dot(ds, qkv_s[0, rows], TN) * mask
            acc[2, rows] += dot(p.astype(BF16), dm, TN)
        return 0

    lax.fori_loop(0, HEADS, head, 0)
    hat, scale = norm(x.astype(F32))
    normed = hat.astype(BF16)
    dn = None
    for t in range(3):
        d = acc[t].astype(BF16)
        grads[first + t] = dot(normed, d, TN).astype(BF16)
        part = dot(d, qkv[:, t * E:(t + 1) * E], NT)
        dn = part if dn is None else dn + part
    return (g.astype(F32) + norm_back(hat, scale, dn.astype(BF16).astype(F32))).astype(BF16)


def unpack_kernel(cells, cotangent, where, c_out, g_out, flat):
    rows = cells.shape[0]
    for a in range(cells.shape[1] // E):
        flat[a * rows:(a + 1) * rows] = cells[:, a * E:(a + 1) * E].astype(F32)
    c_out[...] = moved(where, flat[...].astype(BF16)).astype(BF16)
    for a in range(cells.shape[1] // E):
        flat[a * rows:(a + 1) * rows] = cotangent[:, a * E:(a + 1) * E].astype(F32)
    g_out[...] = flat[...].astype(BF16)


def attr_kernel(n, size, tokens, where_in, where_out, qkv, out, send, x_out, mixed_out, qkv_s, p_s, acc):
    x_out[...] = moved(where_in, tokens[...]).astype(BF16)
    _, mixed, result = attend(x_out, qkv, out[...], qkv_s, p_s, acc, n, size, None)
    mixed_out[...] = mixed
    send[...] = moved(where_out, result).astype(BF16)


def attr_back_kernel(n, size, tokens, where, x, mixed, qkv_s, p_s, qkv, out, send, grads, acc, dm_s):
    g = moved(where, tokens[...]).astype(BF16)
    send[...] = attend_back(
        x[...], g, mixed[...], qkv, out[...], qkv_s, p_s, acc, dm_s, grads, 0, n, size
    )


def middle_kernel(
    n, size, length, tokens, cots, where_x, where_g, where_back, split, qkv, out, up, down,
    send, grads, x_s, g_s, qkv_s, p_s, acc, dm_s, dn_s, bias,
):
    x_s[...] = moved(where_x, tokens[...]).astype(BF16)
    g_s[...] = moved(where_g, cots[...]).astype(BF16)
    row = lax.broadcasted_iota(jnp.int32, (size, size), 0)
    column = lax.broadcasted_iota(jnp.int32, (size, size), 1)
    same = None
    for s in range(size // length):
        low, high = s * length, (s + 1) * length
        inside = (row >= low) & (row < high) & (column >= low) & (column < high)
        same = inside if same is None else same | inside
    bias[...] = jnp.where(same & (split[...] > 0), 1.0, 0.0)
    _, mixed, second = attend(x_s, qkv, out[...], qkv_s, p_s, acc, n, size, bias)
    hat, scale = norm(second.astype(F32))
    normed = hat.astype(BF16)
    g = g_s[...]
    for c in range(up.shape[1] // E):
        w_up = up[:, c * E:(c + 1) * E]
        pre = dot(normed, w_up)
        cdf = 0.5 * (1.0 + lax.erf(pre * (1.0 / math.sqrt(2.0))))
        hidden = (pre * cdf).astype(BF16)
        slope = cdf + pre * (jnp.exp(pre * pre * -0.5) * (1.0 / math.sqrt(2.0 * math.pi)))
        dh = dot(g, down[c * E:(c + 1) * E], NT).astype(BF16).astype(F32)
        dpre = (dh * slope).astype(BF16)
        grads[4 + c] = dot(normed, dpre, TN).astype(BF16)
        grads[8 + c] = dot(hidden, g, TN).astype(BF16)
        part = dot(dpre, w_up, NT)
        if c == 0:
            dn_s[...] = part
        else:
            dn_s[...] += part
    dn = dn_s[...].astype(BF16).astype(F32)
    g = (g.astype(F32) + norm_back(hat, scale, dn)).astype(BF16)
    result = attend_back(
        x_s[...], g, mixed, qkv, out[...], qkv_s, p_s, acc, dm_s, grads, 0, n, size
    )
    send[...] = moved(where_back, result).astype(BF16)


def finish_kernel(factor, tokens, where, total, cells, qa, oa, qs, os, gu, gd, flat):
    rows = cells.shape[0]
    flat[...] = moved(where, tokens[...])
    for a in range(0, cells.shape[1] // E, 2):
        pair = [flat[(a + k) * rows:(a + k + 1) * rows] for k in range(2)]
        cells[:, a * E:(a + 2) * E] = jnp.concatenate(pair, axis=1).astype(BF16)

    def block(b):
        return total[b].astype(F32) * factor

    for ref, start in ((qs, 0), (qa, 12)):
        ref[...] = jnp.concatenate([block(start + t) for t in range(3)], axis=1)
    os[...] = block(3)
    oa[...] = block(15)
    gu[...] = jnp.concatenate([block(4 + c) for c in range(4)], axis=1)
    for c in range(4):
        gd[c * E:(c + 1) * E] = block(8 + c)


def greet(peers):
    barrier = pltpu.get_barrier_semaphore()
    for peer in peers:
        pl.semaphore_signal(barrier, inc=1, device_id=peer, device_id_type=MESH)
    pl.semaphore_wait(barrier, len(peers))


def position(axes):
    return tuple(lax.axis_index(a) for a in axes)


def shifts_of(axes):
    sizes = [lax.axis_size(a) for a in axes]
    return [s for s in np.ndindex(*sizes) if any(s)], sizes


def start_swap(axes, src, dst, send_sem, recv_sem):
    shifts, sizes = shifts_of(axes)
    me = position(axes)
    copies = []
    for k, shift in enumerate(shifts):
        to = tuple(lax.rem(m + d, n) for m, d, n in zip(me, shift, sizes))
        copy = pltpu.make_async_remote_copy(
            src_ref=src.at[to],
            dst_ref=dst.at[me],
            send_sem=send_sem.at[k],
            recv_sem=recv_sem.at[k],
            device_id=dict(zip(axes, to)),
            device_id_type=MESH,
        )
        copy.start()
        copies.append(copy)
    dst[me] = src[me]
    return copies


def peers_of(axes):
    shifts, sizes = shifts_of(axes)
    me = position(axes)
    return [
        dict(zip(axes, (lax.rem(m + d, n) for m, d, n in zip(me, s, sizes)))) for s in shifts
    ]


def swap_kernel(flows, *refs):
    n = len(flows)
    ins, outs, sems = refs[:n], refs[n:2 * n], refs[2 * n:]
    greeted = []
    names = []
    for axes in flows:
        if axes not in names:
            names.append(axes)
            greeted += peers_of(axes)
    greet(greeted)
    copies = []
    for f, axes in enumerate(flows):
        copies += start_swap(axes, ins[f], outs[f], sems[2 * f], sems[2 * f + 1])
    for copy in copies:
        copy.wait()


def swap(flows, arrays, number):
    counts = [math.prod(lax.axis_size(a) for a in axes) for axes in flows]
    return pl.pallas_call(
        functools.partial(swap_kernel, flows),
        out_shape=[jax.ShapeDtypeStruct(a.shape, a.dtype) for a in arrays],
        in_specs=[VMEM] * len(arrays),
        out_specs=[VMEM] * len(arrays),
        scratch_shapes=[pltpu.SemaphoreType.DMA((c,)) for c in counts for _ in range(2)],
        compiler_params=pltpu.CompilerParams(collective_id=number, has_side_effects=True),
    )(*arrays)


def total_kernel(cells, buf, cells_out, out, r1, r2, r3, s1, s2, c_send, c_recv, sems):
    rec, attr = lax.axis_index("rec"), lax.axis_index("attr")
    n_rec, n_attr = lax.axis_size("rec"), lax.axis_size("attr")
    n_x = n_attr // 2
    half, x = lax.rem(attr, 2), lax.div(attr, 2)
    h1 = buf.shape[0] // 2
    h2 = h1 // n_x
    base = half * h1 + x * h2
    greet(peers_of(("attr",)) + peers_of(("rec",)))
    sem = iter(range(1000))

    def push(src, dst, device):
        k = next(sem)
        copy = pltpu.make_async_remote_copy(
            src_ref=src, dst_ref=dst, send_sem=sems.at[0, k], recv_sem=sems.at[1, k],
            device_id=device, device_id_type=MESH,
        )
        copy.start()
        return copy

    def settle(copies):
        for copy in copies:
            copy.wait()

    partner = {"attr": x * 2 + 1 - half}
    columns = [lax.rem(x + d, n_x) for d in range(1, n_x)]
    lines = [lax.rem(rec + d, n_rec) for d in range(1, n_rec)]
    first = [push(buf.at[pl.ds((1 - half) * h1, h1)], r1, partner)]
    swaps = start_swap(("attr",), cells, cells_out, c_send, c_recv)
    settle(first)
    for b in range(h1):
        s1[b] = (buf[half * h1 + b].astype(F32) + r1[b].astype(F32)).astype(BF16)
    settle([
        push(s1.at[pl.ds(c * h2, h2)], r2.at[d], {"attr": c * 2 + half}) for d, c in enumerate(columns)
    ])
    for b in range(h2):
        value = s1[x * h2 + b].astype(F32)
        for d in range(n_x - 1):
            value += r2[d, b].astype(F32)
        s2[b] = value.astype(BF16)
    settle([push(s2.at[:, r], r3.at[d], {"rec": r}) for d, r in enumerate(lines)])
    for b in range(h2):
        value = s2[b, rec].astype(F32)
        for d in range(n_rec - 1):
            value += r3[d, b].astype(F32)
        out[base + b, rec] = value.astype(BF16)
    own = out.at[pl.ds(base, h2), rec]
    settle([push(own, own, {"rec": r}) for r in lines])
    own = out.at[pl.ds(base, h2)]
    settle([push(own, own, {"attr": c * 2 + half}) for c in columns])
    own = out.at[pl.ds(half * h1, h1)]
    settle([push(own, own, partner)])
    settle(swaps)


def local(
    cells, cotangent, qkv_attr, out_attr, qkv_samp, out_samp, up_weight, down_weight, train_split
):
    n_rec, n_attr = lax.axis_size("rec"), lax.axis_size("attr")
    rows, cols = cells.shape[0], cells.shape[1] // E
    tokens = rows * cols
    width = cols * n_attr
    length = rows * n_rec
    few = rows // n_attr
    thin = cols // n_rec
    n_a = tokens // width
    size = length * max(1, min(256 // length, thin))
    n_s = tokens // size

    def shape(*dims, dtype=BF16):
        return jax.ShapeDtypeStruct(dims, dtype)

    def call(kernel, outs, scratch, *args):
        return pl.pallas_call(
            kernel,
            out_shape=outs,
            in_specs=[VMEM] * len(args),
            out_specs=[VMEM] * len(outs),
            scratch_shapes=scratch,
            compiler_params=pltpu.CompilerParams(vmem_limit_bytes=48 * 2**20),
        )(*args)

    flat = [pltpu.VMEM((tokens, E), F32)]
    table = shape(tokens, E)
    acc = pltpu.VMEM((3, tokens, E), F32)
    tall = pltpu.VMEM((tokens, E), BF16)

    c_send, g_send = call(
        unpack_kernel, [table, table], flat, cells, cotangent, place((cols, rows), (1, 0))
    )
    c_got, g_got = swap(
        (("attr",), ("rec",)),
        [c_send.reshape(n_attr, -1, E), g_send.reshape(n_rec, -1, E)],
        0,
    )
    spread = place((few, n_attr, n_rec, thin), (2, 1, 0, 3))
    gathered = place((n_rec, n_attr, few, thin), (2, 1, 0, 3))
    f_send, x_attr, mixed_attr, qkv_kept, p_kept = call(
        functools.partial(attr_kernel, n_a, width),
        [table, table, table, shape(3, tokens, E), shape(n_a, HEADS, width, width, dtype=F32)],
        [acc],
        c_got.reshape(tokens, E), place((n_attr, few, cols), (1, 0, 2)), spread, qkv_attr, out_attr,
    )
    split = (n_rec, n_attr, few * thin, E)
    (f_got,) = swap((("rec", "attr"),), [f_send.reshape(split)], 1)
    back, grads_middle = call(
        functools.partial(middle_kernel, n_s, size, length),
        [table, shape(12, E, E)],
        [
            tall, tall, pltpu.VMEM((3, tokens, E), BF16), pltpu.VMEM((n_s, HEADS, size, size), F32),
            acc, tall, pltpu.VMEM((tokens, E), F32), pltpu.VMEM((size, size), F32),
        ],
        f_got.reshape(tokens, E), g_got.reshape(tokens, E),
        place((length, thin), (1, 0)),
        place((n_rec, thin, rows), (1, 0, 2)),
        place((thin, length), (1, 0)),
        jnp.tile(train_split, size // length)[None, :],
        qkv_samp, out_samp, up_weight, down_weight,
    )
    (b_got,) = swap((("rec", "attr"),), [back.reshape(split)], 2)
    last, grads_attr = call(
        functools.partial(attr_back_kernel, n_a, width),
        [table, shape(4, E, E)],
        [acc, tall],
        b_got.reshape(tokens, E), gathered, x_attr, mixed_attr, qkv_kept, p_kept, qkv_attr, out_attr,
    )
    last = moved_out(last, few, n_attr, cols)
    grads = jnp.concatenate([grads_middle, grads_attr], axis=0)
    part = E // n_rec
    h1 = BLOCKS // 2
    h2 = h1 // (n_attr // 2)
    o_got, totals = pl.pallas_call(
        total_kernel,
        out_shape=[shape(n_attr, few, cols, E), shape(BLOCKS, n_rec, part, E)],
        in_specs=[VMEM] * 2,
        out_specs=[VMEM] * 2,
        scratch_shapes=[
            pltpu.VMEM((h1, n_rec, part, E), BF16),
            pltpu.VMEM((max(1, n_attr // 2 - 1), h2, n_rec, part, E), BF16),
            pltpu.VMEM((max(1, n_rec - 1), h2, part, E), BF16),
            pltpu.VMEM((h1, n_rec, part, E), BF16),
            pltpu.VMEM((h2, n_rec, part, E), BF16),
            pltpu.SemaphoreType.DMA((n_attr,)),
            pltpu.SemaphoreType.DMA((n_attr,)),
            pltpu.SemaphoreType.DMA((2, 2 * (n_rec + n_attr // 2))),
        ],
        compiler_params=pltpu.CompilerParams(collective_id=3, has_side_effects=True),
    )(last, grads.reshape(BLOCKS, n_rec, part, E))
    factor = 1.0 / math.sqrt(length * width)
    out = call(
        functools.partial(finish_kernel, factor),
        [
            shape(rows, cols * E), shape(E, 3 * E, dtype=F32), shape(E, E, dtype=F32),
            shape(E, 3 * E, dtype=F32), shape(E, E, dtype=F32),
            shape(E, 4 * E, dtype=F32), shape(4 * E, E, dtype=F32),
        ],
        flat,
        o_got.reshape(tokens, E), place((rows, cols), (1, 0)), totals.reshape(BLOCKS, E, E),
    )
    return tuple(out)


def moved_out(last, few, n_attr, cols):
    return last.reshape(few, n_attr, cols, E).swapaxes(0, 1)


def solution(mesh):
    both = P(("groups", "rec"), "attr")
    in_specs = (both, both, P(), P(), P(), P(), P(), P(), P("groups"))
    out_specs = (both,) + (P("groups", None),) * 6
    return jax.shard_map(local, mesh=mesh, in_specs=in_specs, out_specs=out_specs, check_vma=False)
```

```python
import functools
import math

import jax
import jax.numpy as jnp
import numpy as np
from jax import lax
from jax.experimental import pallas as pl
from jax.experimental.pallas import tpu as pltpu
from jax.sharding import PartitionSpec as P

E = 192
HEADS = 6
HD = E // HEADS
SCALE = 1.0 / math.sqrt(HD)
BLOCKS = 16
F32 = jnp.float32
BF16 = jnp.bfloat16
MESH = pl.DeviceIdType.MESH
NN = (((1,), (0,)), ((), ()))
NT = (((1,), (1,)), ((), ()))
TN = (((0,), (0,)), ((), ()))
VMEM = pl.BlockSpec(memory_space=pltpu.VMEM)
ANY = pl.BlockSpec(memory_space=pl.ANY)


def dot(a, b, form=NN):
    return lax.dot_general(a, b, form, preferred_element_type=F32)


def place(sizes, order):
    index = np.arange(math.prod(sizes)).reshape(sizes).transpose(order).reshape(-1)
    there = np.empty_like(index)
    there[index] = np.arange(index.size)
    return there.astype(np.int32)


def moved(where_ref, x):
    n = x.shape[0]
    hot = lax.broadcasted_iota(jnp.int32, (n, n), 0) == where_ref[...]
    return dot(jnp.where(hot, 1.0, 0.0).astype(BF16), x)


def put(ref, b, value):
    pieces, part = ref.shape[1], ref.shape[2]
    side = jnp.concatenate([value[: E // 2], value[E // 2:]], axis=1)
    for r in range(pieces):
        ref[b, r] = side[r * part:(r + 1) * part].astype(BF16)


def pack(ref, value, few):
    run = value.shape[0] // few
    pieces, part = ref.shape[0], ref.shape[1]
    side = jnp.concatenate([value[k * run:(k + 1) * run] for k in range(few)], axis=1)
    for r in range(pieces):
        ref[r] = side[r * part:(r + 1) * part].astype(BF16)


def unpack(ref, flat, few):
    pieces, part = ref.shape[0], ref.shape[1]
    run = pieces * part
    for r in range(pieces):
        side = ref[r].astype(F32)
        for k in range(few):
            flat[k * run + r * part:k * run + (r + 1) * part] = side[:, k * E:(k + 1) * E]
    return flat[...].astype(BF16)


def norm(x):
    center = x - jnp.mean(x, axis=-1, keepdims=True)
    scale = lax.rsqrt(jnp.mean(center * center, axis=-1, keepdims=True) + 1e-05)
    return center * scale, scale


def norm_back(hat, scale, grad):
    return scale * (
        grad
        - jnp.mean(grad, axis=-1, keepdims=True)
        - hat * jnp.mean(grad * hat, axis=-1, keepdims=True)
    )


def head_mask(h):
    lane = lax.broadcasted_iota(jnp.int32, (1, E), 1)
    return jnp.where((lane >= h * HD) & (lane < (h + 1) * HD), 1.0, 0.0).astype(F32)


def attend(x_ref, qkv, out, qkv_s, p_s, acc, n, size, bias):
    normed = norm(x_ref[...].astype(F32))[0].astype(BF16)
    for t in range(3):
        qkv_s[t] = dot(normed, qkv[:, t * E:(t + 1) * E]).astype(BF16)
    acc[0] = jnp.zeros(acc.shape[1:], F32)

    def head(h, _):
        mask = head_mask(h)
        for b in range(n):
            rows = pl.ds(b * size, size)
            s = dot(qkv_s[0, rows] * mask.astype(BF16), qkv_s[1, rows], NT) * SCALE
            if bias is not None:
                s = jnp.where(bias[...] > 0, s, -1e30)
            e = jnp.exp(s - jnp.max(s, axis=-1, keepdims=True))
            p = e * (1.0 / jnp.sum(e, axis=-1, keepdims=True))
            p_s[b, h] = p
            acc[0, rows] += dot(p.astype(BF16), qkv_s[2, rows]) * mask
        return 0

    lax.fori_loop(0, HEADS, head, 0)
    mixed = acc[0].astype(BF16)
    return normed, mixed, (x_ref[...].astype(F32) + dot(mixed, out)).astype(BF16)


def attend_back(x, g, mixed, qkv, out, qkv_s, p_s, acc, dm_s, grads, first, n, size):
    dm_s[...] = dot(g, out, NT).astype(BF16)
    put(grads, first + 3, dot(mixed, g, TN))
    acc[...] = jnp.zeros(acc.shape, F32)

    def head(h, _):
        mask = head_mask(h)
        for b in range(n):
            rows = pl.ds(b * size, size)
            dm = dm_s[rows] * mask.astype(BF16)
            p = p_s[b, h]
            dp = dot(dm, qkv_s[2, rows], NT).astype(BF16).astype(F32)
            ds = (p * (dp - jnp.sum(dp * p, axis=-1, keepdims=True)) * SCALE).astype(BF16)
            acc[0, rows] += dot(ds, qkv_s[1, rows]) * mask
            acc[1, rows] += dot(ds, qkv_s[0, rows], TN) * mask
            acc[2, rows] += dot(p.astype(BF16), dm, TN)
        return 0

    lax.fori_loop(0, HEADS, head, 0)
    hat, scale = norm(x.astype(F32))
    normed = hat.astype(BF16)
    dn = None
    for t in range(3):
        d = acc[t].astype(BF16)
        put(grads, first + t, dot(normed, d, TN))
        part = dot(d, qkv[:, t * E:(t + 1) * E], NT)
        dn = part if dn is None else dn + part
    return (g.astype(F32) + norm_back(hat, scale, dn.astype(BF16).astype(F32))).astype(BF16)


def rows_of(cells, flat):
    rows = cells.shape[0]
    for a in range(cells.shape[1] // E):
        flat[a * rows:(a + 1) * rows] = cells[:, a * E:(a + 1) * E].astype(F32)
    return flat[...].astype(BF16)


def shifts_of(axes):
    sizes = [lax.axis_size(a) for a in axes]
    return [s for s in np.ndindex(*sizes) if any(s)], sizes


def peers_of(axes):
    shifts, sizes = shifts_of(axes)
    me = [lax.axis_index(a) for a in axes]
    return [[lax.rem(m + d, n) for m, d, n in zip(me, s, sizes)] for s in shifts]


def start_swap(axes, src, dst, sems):
    _, sizes = shifts_of(axes)

    def flat(where):
        number = where[0]
        for w, n in zip(where[1:], sizes[1:]):
            number = number * n + w
        return number

    me = flat([lax.axis_index(a) for a in axes])
    copies = []
    for k, to in enumerate(peers_of(axes)):
        copy = pltpu.make_async_remote_copy(
            src_ref=src.at[flat(to)],
            dst_ref=dst.at[me],
            send_sem=sems.at[0, k],
            recv_sem=sems.at[1, k],
            device_id=dict(zip(axes, to)),
            device_id_type=MESH,
        )
        copy.start()
        copies.append(copy)
    dst[me] = src[me]
    return copies


def settle(copies):
    for copy in copies:
        copy.wait()


def total_steps(buf, out, first, count, r1, r2, r3, s1, s2, sems):
    rec, attr = lax.axis_index("rec"), lax.axis_index("attr")
    n_rec, n_x = lax.axis_size("rec"), lax.axis_size("attr") // 2
    half, x = lax.rem(attr, 2), lax.div(attr, 2)
    h1 = count // 2
    h2 = h1 // n_x
    base = first + half * h1 + x * h2
    sem = iter(range(sems.shape[1]))

    def push(src, dst, device):
        k = next(sem)
        copy = pltpu.make_async_remote_copy(
            src_ref=src, dst_ref=dst, send_sem=sems.at[0, k], recv_sem=sems.at[1, k],
            device_id=device, device_id_type=MESH,
        )
        copy.start()
        return copy

    partner = {"attr": x * 2 + 1 - half}
    columns = [lax.rem(x + d, n_x) for d in range(1, n_x)]
    lines = [lax.rem(rec + d, n_rec) for d in range(1, n_rec)]
    copies = [push(buf.at[pl.ds(first + (1 - half) * h1, h1)], r1, partner)]
    yield
    settle(copies)
    for b in range(h1):
        s1[b] = (buf[first + half * h1 + b].astype(F32) + r1[b].astype(F32)).astype(BF16)
    copies = [
        push(s1.at[pl.ds(c * h2, h2)], r2.at[d], {"attr": c * 2 + half}) for d, c in enumerate(columns)
    ]
    yield
    settle(copies)
    for b in range(h2):
        value = s1[x * h2 + b].astype(F32)
        for d in range(n_x - 1):
            value += r2[d, b].astype(F32)
        s2[b] = value.astype(BF16)
    copies = [push(s2.at[:, r], r3.at[d], {"rec": r}) for d, r in enumerate(lines)]
    yield
    settle(copies)
    for b in range(h2):
        value = s2[b, rec].astype(F32)
        for d in range(n_rec - 1):
            value += r3[d, b].astype(F32)
        out[base + b, rec] = value.astype(BF16)
    own = out.at[pl.ds(base, h2), rec]
    copies = [push(own, own, {"rec": r}) for r in lines]
    yield
    settle(copies)
    own = out.at[pl.ds(base, h2)]
    copies = [push(own, own, {"attr": c * 2 + half}) for c in columns]
    yield
    settle(copies)
    own = out.at[pl.ds(first + half * h1, h1)]
    copies = [push(own, own, partner)]
    yield
    settle(copies)
    yield


COUNTS = (8, 4, 4)


def layer_kernel(
    size_a, size_s, length, few,
    cells_h, cot_h, qkva_h, outa_h, qkvs_h, outs_h, up_h, down_h, split_h, place_h,
    o_got, totals,
    cells, cot, qkva, outa, qkvs, outs, up, down, split, places, in_sems,
    flat, c_send, c_got, g_send, g_got, f_send, f_got, b_send, b_got, o_send,
    x_a, mixed_a, qkv_a, p_a, x_s, g_s, qkv_s, p_s, acc, dm_s, dn_s, bias, grads,
    c_sems, g_sems, f_sems, b_sems, o_sems, *sums,
):
    tokens = flat.shape[0]
    n_a, n_s = tokens // size_a, tokens // size_s
    loads = {}
    pairs = (
        (cells_h, cells), (place_h, places), (cot_h, cot), (qkva_h, qkva), (outa_h, outa),
        (split_h, split), (qkvs_h, qkvs), (outs_h, outs), (up_h, up), (down_h, down),
    )
    for k, (src, dst) in enumerate(pairs):
        loads[k] = pltpu.make_async_copy(src, dst, in_sems.at[k])
        loads[k].start()
    barrier = pltpu.get_barrier_semaphore()
    peers = peers_of(("rec", "attr"))
    for r, a in peers:
        pl.semaphore_signal(barrier, inc=1, device_id={"rec": r, "attr": a}, device_id_type=MESH)

    def at(k):
        return places.at[k:k + 1]

    loads[0].wait()
    loads[1].wait()
    pack(c_send, moved(at(0), rows_of(cells, flat)), few)
    pl.semaphore_wait(barrier, len(peers))
    c_copies = start_swap(("attr",), c_send, c_got, c_sems)
    loads[2].wait()
    pack(g_send, moved(at(1), rows_of(cot, flat)), few)
    g_copies = start_swap(("rec",), g_send, g_got, g_sems)
    for k in range(3, len(pairs)):
        loads[k].wait()
    settle(c_copies)
    x_a[...] = unpack(c_got, flat, few)
    _, mixed, first = attend(x_a, qkva, outa[...], qkv_a, p_a, acc, n_a, size_a, None)
    mixed_a[...] = mixed
    pack(f_send, moved(at(2), first), few)
    f_copies = start_swap(("rec", "attr"), f_send, f_got, f_sems)

    row = lax.broadcasted_iota(jnp.int32, (size_s, size_s), 0)
    column = lax.broadcasted_iota(jnp.int32, (size_s, size_s), 1)
    same = None
    for s in range(size_s // length):
        low, high = s * length, (s + 1) * length
        inside = (row >= low) & (row < high) & (column >= low) & (column < high)
        same = inside if same is None else same | inside
    bias[...] = jnp.where(same, split[...].astype(F32), 0.0)
    settle(g_copies)
    g_s[...] = moved(at(4), unpack(g_got, flat, few)).astype(BF16)
    settle(f_copies)
    x_s[...] = moved(at(3), unpack(f_got, flat, few)).astype(BF16)
    _, mixed, second = attend(x_s, qkvs, outs[...], qkv_s, p_s, acc, n_s, size_s, bias)
    hat, scale = norm(second.astype(F32))
    normed = hat.astype(BF16)
    g = g_s[...]
    for c in range(up.shape[1] // E):
        w_up = up[:, c * E:(c + 1) * E]
        pre = dot(normed, w_up)
        cdf = 0.5 * (1.0 + lax.erf(pre * (1.0 / math.sqrt(2.0))))
        hidden = (pre * cdf).astype(BF16)
        slope = cdf + pre * (jnp.exp(pre * pre * -0.5) * (1.0 / math.sqrt(2.0 * math.pi)))
        dh = dot(g, down[c * E:(c + 1) * E], NT).astype(BF16).astype(F32)
        dpre = (dh * slope).astype(BF16)
        put(grads, c, dot(normed, dpre, TN))
        put(grads, 4 + c, dot(hidden, g, TN))
        part = dot(dpre, w_up, NT)
        if c == 0:
            dn_s[...] = part
        else:
            dn_s[...] += part
    starts = (0, COUNTS[0], COUNTS[0] + COUNTS[1])
    ffn, samp, attr = (
        total_steps(grads, totals, starts[k], COUNTS[k], *sums[6 * k:6 * k + 6]) for k in range(3)
    )
    next(ffn)
    dn = dn_s[...].astype(BF16).astype(F32)
    g = (g.astype(F32) + norm_back(hat, scale, dn)).astype(BF16)
    back = attend_back(
        x_s[...], g, mixed, qkvs, outs[...], qkv_s, p_s, acc, dm_s, grads, starts[1], n_s, size_s
    )
    pack(b_send, moved(at(5), back), few)
    b_copies = start_swap(("rec", "attr"), b_send, b_got, b_sems)
    next(samp)
    next(ffn)
    settle(b_copies)
    next(samp)
    next(ffn)
    g = moved(at(6), unpack(b_got, flat, few)).astype(BF16)
    back = attend_back(
        x_a[...], g, mixed_a[...], qkva, outa[...], qkv_a, p_a, acc, dm_s, grads, starts[2], n_a, size_a
    )
    pack(o_send, back.astype(F32), few)
    o_copies = start_swap(("attr",), o_send, o_got, o_sems)
    next(attr)
    for steps in (ffn, samp, attr, ffn, samp, attr, ffn, samp, attr, ffn, samp, attr, samp, attr, attr):
        next(steps)
    settle(o_copies)


def finish_kernel(
    factor, few, tokens_h, places_h, total_h, cells, qa, oa, qs, os, gu, gd,
    tokens, places, total, sems, flat, out_flat, tmp,
):
    loads = [
        pltpu.make_async_copy(src, dst, sems.at[k])
        for k, (src, dst) in enumerate(((tokens_h, tokens), (places_h, places), (total_h, total)))
    ]
    for load in loads:
        load.start()
    rows = cells.shape[0]
    loads[0].wait()
    loads[1].wait()
    out_flat[...] = moved(places.at[7:8], unpack(tokens, flat, few))
    for a in range(0, cells.shape[1] // E, 2):
        pair = [out_flat[(a + k) * rows:(a + k + 1) * rows] for k in range(2)]
        cells[:, a * E:(a + 2) * E] = jnp.concatenate(pair, axis=1).astype(BF16)
    loads[2].wait()

    def block(b):
        part = total.shape[2]
        for r in range(total.shape[1]):
            tmp[b, r * part:(r + 1) * part] = total[b, r].astype(F32) * factor
        side = tmp[b]
        return jnp.concatenate([side[:, :E], side[:, E:]], axis=0)

    gu[...] = jnp.concatenate([block(c) for c in range(4)], axis=1)
    for c in range(4):
        gd[c * E:(c + 1) * E] = block(4 + c)
    for ref, start in ((qs, 8), (qa, 12)):
        ref[...] = jnp.concatenate([block(start + t) for t in range(3)], axis=1)
    os[...] = block(11)
    oa[...] = block(15)


def local(
    cells, cotangent, qkv_attr, out_attr, qkv_samp, out_samp, up_weight, down_weight, train_split
):
    n_rec, n_attr = lax.axis_size("rec"), lax.axis_size("attr")
    rows, cols = cells.shape[0], cells.shape[1] // E
    tokens = rows * cols
    width = cols * n_attr
    length = rows * n_rec
    few = rows // n_attr
    thin = cols // n_rec
    size = length * max(1, min(256 // length, thin))
    places = jnp.asarray(np.stack([
        place((cols, n_attr, few), (2, 1, 0)),
        place((n_rec, thin, n_attr, few), (3, 0, 1, 2)),
        place((few, n_attr, n_rec, thin), (0, 2, 1, 3)),
        place((few, n_rec, n_attr, thin), (3, 1, 2, 0)),
        place((few, n_rec, thin, n_attr), (2, 1, 3, 0)),
        place((thin, n_rec, n_attr, few), (3, 1, 2, 0)),
        place((few, n_rec, n_attr, thin), (0, 2, 1, 3)),
        place((few, n_attr, cols), (2, 1, 0)),
    ]))
    split = jnp.tile(train_split, size // length)[None, :]
    all_devices = n_rec * n_attr
    part = E // 2 // n_rec
    n_x = n_attr // 2

    def shape(*dims, dtype=BF16):
        return jax.ShapeDtypeStruct(dims, dtype)

    def vmem(*dims, dtype=BF16):
        return pltpu.VMEM(dims, dtype)

    args = (
        cells, cotangent, qkv_attr, out_attr, qkv_samp, out_samp, up_weight, down_weight, split, places
    )
    c_buf = vmem(n_attr, cols, few * E)
    g_buf = vmem(n_rec, thin * n_attr, few * E)
    f_buf = vmem(all_devices, thin, few * E)
    table = vmem(tokens, E)
    sums = []
    for count in COUNTS:
        h1 = count // 2
        h2 = h1 // n_x
        sums += [
            vmem(h1, n_rec, part, 2 * E), vmem(max(1, n_x - 1), h2, n_rec, part, 2 * E),
            vmem(max(1, n_rec - 1), h2, part, 2 * E), vmem(h1, n_rec, part, 2 * E),
            vmem(h2, n_rec, part, 2 * E),
            pltpu.SemaphoreType.DMA((2, 2 * (n_rec + n_x - 1))),
        ]
    o_got, totals = pl.pallas_call(
        functools.partial(layer_kernel, width, size, length, few),
        out_shape=[shape(n_attr, cols, few * E), shape(BLOCKS, n_rec, part, 2 * E)],
        in_specs=[ANY] * len(args),
        out_specs=[VMEM] * 2,
        scratch_shapes=[pltpu.VMEM(a.shape, a.dtype) for a in args]
        + [
            pltpu.SemaphoreType.DMA((len(args),)),
            vmem(tokens, E, dtype=F32), c_buf, c_buf, g_buf, g_buf, f_buf, f_buf, f_buf, f_buf, c_buf,
            table, table, vmem(3, tokens, E), vmem(tokens // width, HEADS, width, width, dtype=F32),
            table, table, vmem(3, tokens, E), vmem(tokens // size, HEADS, size, size, dtype=F32),
            vmem(3, tokens, E, dtype=F32), table, vmem(tokens, E, dtype=F32),
            vmem(size, size, dtype=F32), vmem(BLOCKS, n_rec, part, 2 * E),
        ]
        + [
            pltpu.SemaphoreType.DMA((2, n))
            for n in (n_attr, n_rec, all_devices, all_devices, n_attr)
        ]
        + sums,
        compiler_params=pltpu.CompilerParams(
            collective_id=0, has_side_effects=True, vmem_limit_bytes=48 * 2**20
        ),
    )(*args)
    outs = [
        shape(rows, cols * E), shape(E, 3 * E, dtype=F32), shape(E, E, dtype=F32),
        shape(E, 3 * E, dtype=F32), shape(E, E, dtype=F32),
        shape(E, 4 * E, dtype=F32), shape(4 * E, E, dtype=F32),
    ]
    last = (o_got, places, totals)
    out = pl.pallas_call(
        functools.partial(finish_kernel, 1.0 / math.sqrt(length * width), few),
        out_shape=outs,
        in_specs=[ANY] * 3,
        out_specs=[VMEM] * len(outs),
        scratch_shapes=[pltpu.VMEM(a.shape, a.dtype) for a in last]
        + [
            pltpu.SemaphoreType.DMA((3,)), vmem(tokens, E, dtype=F32), vmem(tokens, E, dtype=F32),
            vmem(BLOCKS, E // 2, 2 * E, dtype=F32),
        ],
        compiler_params=pltpu.CompilerParams(vmem_limit_bytes=48 * 2**20),
    )(*last)
    return tuple(out)


def solution(mesh):
    both = P(("groups", "rec"), "attr")
    in_specs = (both, both, P(), P(), P(), P(), P(), P(), P("groups"))
    out_specs = (both,) + (P("groups", None),) * 6
    return jax.shard_map(local, mesh=mesh, in_specs=in_specs, out_specs=out_specs, check_vma=False)
```

```python
import functools
import math

import jax
import jax.numpy as jnp
import numpy as np
from jax import lax
from jax.experimental import pallas as pl
from jax.experimental.pallas import tpu as pltpu
from jax.sharding import PartitionSpec as P

E = 192
HEADS = 6
HD = E // HEADS
SCALE = 1.0 / math.sqrt(HD)
BLOCKS = 16
F32 = jnp.float32
BF16 = jnp.bfloat16
MESH = pl.DeviceIdType.MESH
NN = (((1,), (0,)), ((), ()))
NT = (((1,), (1,)), ((), ()))
TN = (((0,), (0,)), ((), ()))
VMEM = pl.BlockSpec(memory_space=pltpu.VMEM)
ANY = pl.BlockSpec(memory_space=pl.ANY)
HBM = pl.BlockSpec(memory_space=pltpu.HBM)


def dot(a, b, form=NN):
    return lax.dot_general(a, b, form, preferred_element_type=F32)


def place(sizes, order):
    index = np.arange(math.prod(sizes)).reshape(sizes).transpose(order).reshape(-1)
    there = np.empty_like(index)
    there[index] = np.arange(index.size)
    return there.astype(np.int32)


def moved(where_ref, x):
    n = x.shape[0]
    hot = lax.broadcasted_iota(jnp.int32, (n, n), 0) == where_ref[...]
    return dot(jnp.where(hot, 1.0, 0.0).astype(BF16), x)


def put(ref, b, value):
    pieces, part = ref.shape[1], ref.shape[2]
    side = jnp.concatenate([value[: E // 2], value[E // 2:]], axis=1)
    for r in range(pieces):
        ref[b, r] = side[r * part:(r + 1) * part].astype(BF16)


def pack(ref, value, few):
    run = value.shape[0] // few
    pieces, part = ref.shape[0], ref.shape[1]
    side = jnp.concatenate([value[k * run:(k + 1) * run] for k in range(few)], axis=1)
    for r in range(pieces):
        ref[r] = side[r * part:(r + 1) * part].astype(BF16)


def unpack(ref, flat, few):
    pieces, part = ref.shape[0], ref.shape[1]
    run = pieces * part
    for r in range(pieces):
        side = ref[r].astype(F32)
        for k in range(few):
            flat[k * run + r * part:k * run + (r + 1) * part] = side[:, k * E:(k + 1) * E]
    return flat[...].astype(BF16)


def norm(x):
    center = x - jnp.mean(x, axis=-1, keepdims=True)
    scale = lax.rsqrt(jnp.mean(center * center, axis=-1, keepdims=True) + 1e-05)
    return center * scale, scale


def norm_back(hat, scale, grad):
    return scale * (
        grad
        - jnp.mean(grad, axis=-1, keepdims=True)
        - hat * jnp.mean(grad * hat, axis=-1, keepdims=True)
    )


def head_mask(h):
    lane = lax.broadcasted_iota(jnp.int32, (1, E), 1)
    return jnp.where((lane >= h * HD) & (lane < (h + 1) * HD), 1.0, 0.0).astype(F32)


def attend(x_ref, qkv, out, qkv_s, p_s, acc, n, size, bias):
    normed = norm(x_ref[...].astype(F32))[0].astype(BF16)
    for t in range(3):
        qkv_s[t] = dot(normed, qkv[:, t * E:(t + 1) * E]).astype(BF16)
    acc[0] = jnp.zeros(acc.shape[1:], F32)

    def head(h, _):
        mask = head_mask(h)
        for b in range(n):
            rows = pl.ds(b * size, size)
            s = dot(qkv_s[0, rows] * mask.astype(BF16), qkv_s[1, rows], NT) * SCALE
            if bias is not None:
                s = jnp.where(bias[...] > 0, s, -1e30)
            e = jnp.exp(s - jnp.max(s, axis=-1, keepdims=True))
            p = e * (1.0 / jnp.sum(e, axis=-1, keepdims=True))
            p_s[b, h] = p
            acc[0, rows] += dot(p.astype(BF16), qkv_s[2, rows]) * mask
        return 0

    lax.fori_loop(0, HEADS, head, 0)
    mixed = acc[0].astype(BF16)
    return normed, mixed, (x_ref[...].astype(F32) + dot(mixed, out)).astype(BF16)


def attend_back(x, g, mixed, qkv, out, qkv_s, p_s, acc, dm_s, grads, first, n, size, between):
    dm_s[...] = dot(g, out, NT).astype(BF16)
    put(grads, first + 3, dot(mixed, g, TN))
    acc[...] = jnp.zeros(acc.shape, F32)

    def head(h, _):
        mask = head_mask(h)
        for b in range(n):
            rows = pl.ds(b * size, size)
            dm = dm_s[rows] * mask.astype(BF16)
            p = p_s[b, h]
            dp = dot(dm, qkv_s[2, rows], NT).astype(BF16).astype(F32)
            ds = (p * (dp - jnp.sum(dp * p, axis=-1, keepdims=True)) * SCALE).astype(BF16)
            acc[0, rows] += dot(ds, qkv_s[1, rows]) * mask
            acc[1, rows] += dot(ds, qkv_s[0, rows], TN) * mask
            acc[2, rows] += dot(p.astype(BF16), dm, TN)
        return 0

    for k, step in enumerate(between):
        lax.fori_loop(k * HEADS // len(between), (k + 1) * HEADS // len(between), head, 0)
        step()
    hat, scale = norm(x.astype(F32))
    normed = hat.astype(BF16)
    dn = None
    for t in range(3):
        d = acc[t].astype(BF16)
        put(grads, first + t, dot(normed, d, TN))
        part = dot(d, qkv[:, t * E:(t + 1) * E], NT)
        dn = part if dn is None else dn + part
    return (g.astype(F32) + norm_back(hat, scale, dn.astype(BF16).astype(F32))).astype(BF16)


def rows_of(cells, flat):
    rows = cells.shape[0]
    for a in range(cells.shape[1] // E):
        flat[a * rows:(a + 1) * rows] = cells[:, a * E:(a + 1) * E].astype(F32)
    return flat[...].astype(BF16)


def shifts_of(axes):
    sizes = [lax.axis_size(a) for a in axes]
    return [s for s in np.ndindex(*sizes) if any(s)], sizes


def peers_of(axes):
    shifts, sizes = shifts_of(axes)
    me = [lax.axis_index(a) for a in axes]
    return [[lax.rem(m + d, n) for m, d, n in zip(me, s, sizes)] for s in shifts]


def start_swap(axes, src, dst, sems):
    _, sizes = shifts_of(axes)

    def flat(where):
        number = where[0]
        for w, n in zip(where[1:], sizes[1:]):
            number = number * n + w
        return number

    me = flat([lax.axis_index(a) for a in axes])
    copies = []
    for k, to in enumerate(peers_of(axes)):
        copy = pltpu.make_async_remote_copy(
            src_ref=src.at[flat(to)],
            dst_ref=dst.at[me],
            send_sem=sems.at[0, k],
            recv_sem=sems.at[1, k],
            device_id=dict(zip(axes, to)),
            device_id_type=MESH,
        )
        copy.start()
        copies.append(copy)
    dst[me] = src[me]
    return copies


def settle(copies):
    for copy in copies:
        copy.wait()


def total_steps(buf, out, first, count, r1, r2, r3, s1, s2, sems):
    rec, attr = lax.axis_index("rec"), lax.axis_index("attr")
    n_rec, n_x = lax.axis_size("rec"), lax.axis_size("attr") // 2
    half, x = lax.rem(attr, 2), lax.div(attr, 2)
    h1 = count // 2
    h2 = h1 // n_x
    base = first + half * h1 + x * h2
    sem = iter(range(sems.shape[1]))

    def push(src, dst, device):
        k = next(sem)
        copy = pltpu.make_async_remote_copy(
            src_ref=src, dst_ref=dst, send_sem=sems.at[0, k], recv_sem=sems.at[1, k],
            device_id=device, device_id_type=MESH,
        )
        copy.start()
        return copy

    partner = {"attr": x * 2 + 1 - half}
    columns = [lax.rem(x + d, n_x) for d in range(1, n_x)]
    lines = [lax.rem(rec + d, n_rec) for d in range(1, n_rec)]
    copies = [push(buf.at[pl.ds(first + (1 - half) * h1, h1)], r1, partner)]
    yield
    settle(copies)
    for b in range(h1):
        s1[b] = (buf[first + half * h1 + b].astype(F32) + r1[b].astype(F32)).astype(BF16)
    copies = [
        push(s1.at[pl.ds(c * h2, h2)], r2.at[d], {"attr": c * 2 + half}) for d, c in enumerate(columns)
    ]
    yield
    settle(copies)
    for b in range(h2):
        value = s1[x * h2 + b].astype(F32)
        for d in range(n_x - 1):
            value += r2[d, b].astype(F32)
        s2[b] = value.astype(BF16)
    copies = [push(s2.at[:, r], r3.at[d], {"rec": r}) for d, r in enumerate(lines)]
    yield
    settle(copies)
    for b in range(h2):
        value = s2[b, rec].astype(F32)
        for d in range(n_rec - 1):
            value += r3[d, b].astype(F32)
        out[base + b, rec] = value.astype(BF16)
    own = out.at[pl.ds(base, h2), rec]
    copies = [push(own, own, {"rec": r}) for r in lines]
    yield
    settle(copies)
    own = out.at[pl.ds(base, h2)]
    copies = [push(own, own, {"attr": c * 2 + half}) for c in columns]
    yield
    settle(copies)
    own = out.at[pl.ds(first + half * h1, h1)]
    copies = [push(own, own, partner)]
    yield
    settle(copies)
    yield


COUNTS = (8, 4, 4)


def layer_kernel(
    size_a, size_s, length, few,
    cells_h, cot_h, qkva_h, outa_h, qkvs_h, outs_h, up_h, down_h, split_h, place_h,
    o_got, totals,
    cells, cot, qkva, outa, qkvs, outs, up, down, split, places, in_sems,
    flat, c_send, c_got, g_send, g_got, f_send, f_got, b_send, b_got, o_send,
    x_a, mixed_a, qkv_a, p_a, x_s, g_s, qkv_s, p_s, acc, dm_s, dn_s, bias, grads,
    c_sems, g_sems, f_sems, b_sems, o_sems, *sums,
):
    tokens = flat.shape[0]
    n_a, n_s = tokens // size_a, tokens // size_s
    loads = {}
    pairs = (
        (cells_h, cells), (place_h, places), (cot_h, cot), (qkva_h, qkva), (outa_h, outa),
        (split_h, split), (qkvs_h, qkvs), (outs_h, outs), (up_h, up), (down_h, down),
    )
    for k, (src, dst) in enumerate(pairs):
        loads[k] = pltpu.make_async_copy(src, dst, in_sems.at[k])
        loads[k].start()
    barrier = pltpu.get_barrier_semaphore()
    peers = peers_of(("rec", "attr"))
    for r, a in peers:
        pl.semaphore_signal(barrier, inc=1, device_id={"rec": r, "attr": a}, device_id_type=MESH)

    def at(k):
        return places.at[k:k + 1]

    loads[0].wait()
    loads[1].wait()
    pack(c_send, moved(at(0), rows_of(cells, flat)), few)
    pl.semaphore_wait(barrier, len(peers))
    c_copies = start_swap(("attr",), c_send, c_got, c_sems)
    loads[2].wait()
    pack(g_send, moved(at(1), rows_of(cot, flat)), few)
    g_copies = start_swap(("rec",), g_send, g_got, g_sems)
    for k in range(3, len(pairs)):
        loads[k].wait()
    settle(c_copies)
    x_a[...] = unpack(c_got, flat, few)
    _, mixed, first = attend(x_a, qkva, outa[...], qkv_a, p_a, acc, n_a, size_a, None)
    mixed_a[...] = mixed
    pack(f_send, moved(at(2), first), few)
    f_copies = start_swap(("rec", "attr"), f_send, f_got, f_sems)

    row = lax.broadcasted_iota(jnp.int32, (size_s, size_s), 0)
    column = lax.broadcasted_iota(jnp.int32, (size_s, size_s), 1)
    same = None
    for s in range(size_s // length):
        low, high = s * length, (s + 1) * length
        inside = (row >= low) & (row < high) & (column >= low) & (column < high)
        same = inside if same is None else same | inside
    tiled = jnp.concatenate([split[...].astype(F32)] * (size_s // length), axis=1)
    bias[...] = jnp.where(same, tiled, 0.0)
    settle(g_copies)
    g_s[...] = moved(at(4), unpack(g_got, flat, few)).astype(BF16)
    settle(f_copies)
    x_s[...] = moved(at(3), unpack(f_got, flat, few)).astype(BF16)
    _, mixed, second = attend(x_s, qkvs, outs[...], qkv_s, p_s, acc, n_s, size_s, bias)
    hat, scale = norm(second.astype(F32))
    normed = hat.astype(BF16)
    g = g_s[...]
    for c in range(up.shape[1] // E):
        w_up = up[:, c * E:(c + 1) * E]
        pre = dot(normed, w_up)
        cdf = 0.5 * (1.0 + lax.erf(pre * (1.0 / math.sqrt(2.0))))
        hidden = (pre * cdf).astype(BF16)
        slope = cdf + pre * (jnp.exp(pre * pre * -0.5) * (1.0 / math.sqrt(2.0 * math.pi)))
        dh = dot(g, down[:, c * E:(c + 1) * E]).astype(BF16).astype(F32)
        dpre = (dh * slope).astype(BF16)
        put(grads, c, dot(normed, dpre, TN))
        put(grads, 4 + c, dot(g, hidden, TN))
        part = dot(dpre, w_up, NT)
        if c == 0:
            dn_s[...] = part
        else:
            dn_s[...] += part
    starts = (0, COUNTS[0], COUNTS[0] + COUNTS[1])
    ffn, samp, attr = (
        total_steps(grads, totals, starts[k], COUNTS[k], *sums[6 * k:6 * k + 6]) for k in range(3)
    )
    next(ffn)
    dn = dn_s[...].astype(BF16).astype(F32)
    g = (g.astype(F32) + norm_back(hat, scale, dn)).astype(BF16)

    def go(*groups):
        def step():
            for group in groups:
                next(group)
        return step

    back = attend_back(
        x_s[...], g, mixed, qkvs, outs[...], qkv_s, p_s, acc, dm_s, grads, starts[1], n_s, size_s,
        (go(ffn), go(), go(ffn)),
    )
    pack(b_send, moved(at(5), back), few)
    b_copies = start_swap(("rec", "attr"), b_send, b_got, b_sems)
    next(samp)
    settle(b_copies)
    go(samp, ffn)()
    g = moved(at(6), unpack(b_got, flat, few)).astype(BF16)
    back = attend_back(
        x_a[...], g, mixed_a[...], qkva, outa[...], qkv_a, p_a, acc, dm_s, grads, starts[2], n_a, size_a,
        (go(ffn), go(samp), go(ffn)),
    )
    next(attr)
    pack(o_send, back.astype(F32), few)
    o_copies = start_swap(("attr",), o_send, o_got, o_sems)
    for steps in (samp, attr, ffn, samp, attr, samp, attr, samp, attr, attr, attr):
        next(steps)
    settle(o_copies)


def finish_kernel(
    factor, few, tokens_h, places_h, total_h, cells, qa, oa, qs, os, gu, gd,
    tokens, places, total, sems, flat, out_flat, tmp,
):
    loads = [
        pltpu.make_async_copy(src, dst, sems.at[k])
        for k, (src, dst) in enumerate(((tokens_h, tokens), (places_h, places), (total_h, total)))
    ]
    for load in loads:
        load.start()
    rows = cells.shape[0]
    loads[0].wait()
    loads[1].wait()
    out_flat[...] = moved(places.at[7:8], unpack(tokens, flat, few))
    for a in range(0, cells.shape[1] // E, 2):
        pair = [out_flat[(a + k) * rows:(a + k + 1) * rows] for k in range(2)]
        cells[:, a * E:(a + 2) * E] = jnp.concatenate(pair, axis=1).astype(BF16)
    loads[2].wait()

    def block(b):
        part = total.shape[2]
        for r in range(total.shape[1]):
            tmp[b, r * part:(r + 1) * part] = total[b, r].astype(F32) * factor
        side = tmp[b]
        return jnp.concatenate([side[:, :E], side[:, E:]], axis=0)

    gu[...] = jnp.concatenate([block(c) for c in range(4)], axis=1)
    gd[...] = jnp.concatenate([block(4 + c) for c in range(4)], axis=1)
    for ref, start in ((qs, 8), (qa, 12)):
        ref[...] = jnp.concatenate([block(start + t) for t in range(3)], axis=1)
    os[...] = block(11)
    oa[...] = block(15)


def local(
    cells, cotangent, qkv_attr, out_attr, qkv_samp, out_samp, up_weight, down_weight, train_split
):
    n_rec, n_attr = lax.axis_size("rec"), lax.axis_size("attr")
    rows, cols = cells.shape[0], cells.shape[1] // E
    tokens = rows * cols
    width = cols * n_attr
    length = rows * n_rec
    few = rows // n_attr
    thin = cols // n_rec
    size = length * max(1, min(256 // length, thin))
    places = jnp.asarray(np.stack([
        place((cols, n_attr, few), (2, 1, 0)),
        place((n_rec, thin, n_attr, few), (3, 0, 1, 2)),
        place((few, n_attr, n_rec, thin), (0, 2, 1, 3)),
        place((few, n_rec, n_attr, thin), (3, 1, 2, 0)),
        place((few, n_rec, thin, n_attr), (2, 1, 3, 0)),
        place((thin, n_rec, n_attr, few), (3, 1, 2, 0)),
        place((few, n_rec, n_attr, thin), (0, 2, 1, 3)),
        place((few, n_attr, cols), (2, 1, 0)),
    ]))
    split = train_split[None, :]
    all_devices = n_rec * n_attr
    part = E // 2 // n_rec
    n_x = n_attr // 2

    def shape(*dims, dtype=BF16):
        return jax.ShapeDtypeStruct(dims, dtype)

    def vmem(*dims, dtype=BF16):
        return pltpu.VMEM(dims, dtype)

    args = (
        cells, cotangent, qkv_attr, out_attr, qkv_samp, out_samp, up_weight, down_weight.T, split, places
    )
    c_buf = vmem(n_attr, cols, few * E)
    g_buf = vmem(n_rec, thin * n_attr, few * E)
    f_buf = vmem(all_devices, thin, few * E)
    table = vmem(tokens, E)
    sums = []
    for count in COUNTS:
        h1 = count // 2
        h2 = h1 // n_x
        sums += [
            vmem(h1, n_rec, part, 2 * E), vmem(max(1, n_x - 1), h2, n_rec, part, 2 * E),
            vmem(max(1, n_rec - 1), h2, part, 2 * E), vmem(h1, n_rec, part, 2 * E),
            vmem(h2, n_rec, part, 2 * E),
            pltpu.SemaphoreType.DMA((2, 2 * (n_rec + n_x - 1))),
        ]
    o_got, totals = pl.pallas_call(
        functools.partial(layer_kernel, width, size, length, few),
        out_shape=[shape(n_attr, cols, few * E), shape(BLOCKS, n_rec, part, 2 * E)],
        in_specs=[HBM] * len(args),
        out_specs=[VMEM] * 2,
        scratch_shapes=[pltpu.VMEM(a.shape, a.dtype) for a in args]
        + [
            pltpu.SemaphoreType.DMA((len(args),)),
            vmem(tokens, E, dtype=F32), c_buf, c_buf, g_buf, g_buf, f_buf, f_buf, f_buf, f_buf, c_buf,
            table, table, vmem(3, tokens, E), vmem(tokens // width, HEADS, width, width, dtype=F32),
            table, table, vmem(3, tokens, E), vmem(tokens // size, HEADS, size, size, dtype=F32),
            vmem(3, tokens, E, dtype=F32), table, vmem(tokens, E, dtype=F32),
            vmem(size, size, dtype=F32), vmem(BLOCKS, n_rec, part, 2 * E),
        ]
        + [
            pltpu.SemaphoreType.DMA((2, n))
            for n in (n_attr, n_rec, all_devices, all_devices, n_attr)
        ]
        + sums,
        compiler_params=pltpu.CompilerParams(
            collective_id=0, has_side_effects=True, vmem_limit_bytes=67043328
        ),
    )(*args)
    outs = [
        shape(rows, cols * E), shape(E, 3 * E, dtype=F32), shape(E, E, dtype=F32),
        shape(E, 3 * E, dtype=F32), shape(E, E, dtype=F32),
        shape(E, 4 * E, dtype=F32), shape(E, 4 * E, dtype=F32),
    ]
    last = (o_got, places, totals)
    out = pl.pallas_call(
        functools.partial(finish_kernel, 1.0 / math.sqrt(length * width), few),
        out_shape=outs,
        in_specs=[ANY] * 3,
        out_specs=[VMEM] * len(outs),
        scratch_shapes=[pltpu.VMEM(a.shape, a.dtype) for a in last]
        + [
            pltpu.SemaphoreType.DMA((3,)), vmem(tokens, E, dtype=F32), vmem(tokens, E, dtype=F32),
            vmem(BLOCKS, E // 2, 2 * E, dtype=F32),
        ],
        compiler_params=pltpu.CompilerParams(vmem_limit_bytes=67043328),
    )(*last)
    return (*out[:6], out[6].T)


def solution(mesh):
    both = P(("groups", "rec"), "attr")
    in_specs = (both, both, P(), P(), P(), P(), P(), P(), P("groups"))
    out_specs = (both,) + (P("groups", None),) * 6
    return jax.shard_map(local, mesh=mesh, in_specs=in_specs, out_specs=out_specs, check_vma=False)
```

```python
import functools
import math

import jax
import jax.numpy as jnp
import numpy as np
from jax import lax
from jax.experimental import pallas as pl
from jax.experimental.pallas import tpu as pltpu
from jax.sharding import PartitionSpec as P

E = 192
HEADS = 6
HD = E // HEADS
SCALE = 1.0 / math.sqrt(HD)
BLOCKS = 16
F32 = jnp.float32
BF16 = jnp.bfloat16
MESH = pl.DeviceIdType.MESH
NN = (((1,), (0,)), ((), ()))
NT = (((1,), (1,)), ((), ()))
TN = (((0,), (0,)), ((), ()))
VMEM = pl.BlockSpec(memory_space=pltpu.VMEM)
ANY = pl.BlockSpec(memory_space=pl.ANY)
HBM = pl.BlockSpec(memory_space=pltpu.HBM)


def dot(a, b, form=NN):
    return lax.dot_general(a, b, form, preferred_element_type=F32)


def place(sizes, order):
    index = np.arange(math.prod(sizes)).reshape(sizes).transpose(order).reshape(-1)
    there = np.empty_like(index)
    there[index] = np.arange(index.size)
    return there.astype(np.int32)


def moved(where_ref, x):
    n = x.shape[0]
    hot = lax.broadcasted_iota(jnp.int32, (n, n), 0) == where_ref[...]
    return dot(jnp.where(hot, 1.0, 0.0).astype(BF16), x)


def put(ref, b, value):
    pieces, part = ref.shape[1], ref.shape[2]
    side = jnp.concatenate([value[: E // 2], value[E // 2:]], axis=1)
    for r in range(pieces):
        ref[b, r] = side[r * part:(r + 1) * part].astype(BF16)


def pack(ref, value, few):
    run = value.shape[0] // few
    pieces, part = ref.shape[0], ref.shape[1]
    side = jnp.concatenate([value[k * run:(k + 1) * run] for k in range(few)], axis=1)
    for r in range(pieces):
        ref[r] = side[r * part:(r + 1) * part].astype(BF16)


def unpack(ref, flat, few):
    pieces, part = ref.shape[0], ref.shape[1]
    run = pieces * part
    for r in range(pieces):
        side = ref[r].astype(F32)
        for k in range(few):
            flat[k * run + r * part:k * run + (r + 1) * part] = side[:, k * E:(k + 1) * E]
    return flat[...].astype(BF16)


def norm(x):
    center = x - jnp.mean(x, axis=-1, keepdims=True)
    scale = lax.rsqrt(jnp.mean(center * center, axis=-1, keepdims=True) + 1e-05)
    return center * scale, scale


def norm_back(hat, scale, grad):
    return scale * (
        grad
        - jnp.mean(grad, axis=-1, keepdims=True)
        - hat * jnp.mean(grad * hat, axis=-1, keepdims=True)
    )


def attend(x_ref, qkv, out, qkv_s, p_s, acc, n, size, bias):
    normed = norm(x_ref[...].astype(F32))[0].astype(BF16)
    for t in range(3):
        qkv_s[t] = dot(normed, qkv[:, t * E:(t + 1) * E]).T.astype(BF16)

    def head(h, _):
        rows = pl.ds(pl.multiple_of(h * HD, HD), HD)
        for b in range(n):
            cols = pl.ds(b * size, size)
            s = dot(qkv_s[1, rows, cols], qkv_s[0, rows, cols], TN) * SCALE
            if bias is not None:
                s = jnp.where(bias[...] > 0, s, -1e30)
            e = jnp.exp(s - jnp.max(s, axis=0, keepdims=True))
            p = e * (1.0 / jnp.sum(e, axis=0, keepdims=True))
            p_s[b, h] = p
            acc[0, rows, cols] = dot(qkv_s[2, rows, cols], p.astype(BF16))
        return 0

    lax.fori_loop(0, HEADS, head, 0)
    mixed = acc[0].T.astype(BF16)
    return normed, mixed, (x_ref[...].astype(F32) + dot(mixed, out)).astype(BF16)


def attend_back(x, g, mixed, qkv, out, qkv_s, p_s, acc, dm_s, grads, first, n, size, between):
    dm_s[...] = dot(out, g, NT).astype(BF16)
    put(grads, first + 3, dot(mixed, g, TN))

    def head(h, _):
        rows = pl.ds(pl.multiple_of(h * HD, HD), HD)
        for b in range(n):
            cols = pl.ds(b * size, size)
            dm = dm_s[rows, cols]
            p = p_s[b, h]
            dp = dot(qkv_s[2, rows, cols], dm, TN).astype(BF16).astype(F32)
            ds = (p * (dp - jnp.sum(dp * p, axis=0, keepdims=True)) * SCALE).astype(BF16)
            acc[0, rows, cols] = dot(qkv_s[1, rows, cols], ds)
            acc[1, rows, cols] = dot(qkv_s[0, rows, cols], ds, NT)
            acc[2, rows, cols] = dot(dm, p.astype(BF16), NT)
        return 0

    for k, step in enumerate(between):
        lax.fori_loop(k * HEADS // len(between), (k + 1) * HEADS // len(between), head, 0)
        step()
    hat, scale = norm(x.astype(F32))
    normed = hat.astype(BF16)
    dn = None
    for t in range(3):
        d = acc[t].T.astype(BF16)
        put(grads, first + t, dot(normed, d, TN))
        part = dot(d, qkv[:, t * E:(t + 1) * E], NT)
        dn = part if dn is None else dn + part
    return (g.astype(F32) + norm_back(hat, scale, dn.astype(BF16).astype(F32))).astype(BF16)


def rows_of(cells, flat):
    rows = cells.shape[0]
    for a in range(cells.shape[1] // E):
        flat[a * rows:(a + 1) * rows] = cells[:, a * E:(a + 1) * E].astype(F32)
    return flat[...].astype(BF16)


def shifts_of(axes):
    sizes = [lax.axis_size(a) for a in axes]
    return [s for s in np.ndindex(*sizes) if any(s)], sizes


def peers_of(axes):
    shifts, sizes = shifts_of(axes)
    me = [lax.axis_index(a) for a in axes]
    return [[lax.rem(m + d, n) for m, d, n in zip(me, s, sizes)] for s in shifts]


def start_swap(axes, src, dst, sems):
    _, sizes = shifts_of(axes)

    def flat(where):
        number = where[0]
        for w, n in zip(where[1:], sizes[1:]):
            number = number * n + w
        return number

    me = flat([lax.axis_index(a) for a in axes])
    copies = []
    for k, to in enumerate(peers_of(axes)):
        copy = pltpu.make_async_remote_copy(
            src_ref=src.at[flat(to)],
            dst_ref=dst.at[me],
            send_sem=sems.at[0, k],
            recv_sem=sems.at[1, k],
            device_id=dict(zip(axes, to)),
            device_id_type=MESH,
        )
        copy.start()
        copies.append(copy)
    dst[me] = src[me]
    return copies


def settle(copies):
    for copy in copies:
        copy.wait()


def total_steps(buf, out, first, count, r1, r2, r3, s1, s2, sems):
    rec, attr = lax.axis_index("rec"), lax.axis_index("attr")
    n_rec, n_x = lax.axis_size("rec"), lax.axis_size("attr") // 2
    half, x = lax.rem(attr, 2), lax.div(attr, 2)
    h1 = count // 2
    h2 = h1 // n_x
    base = first + half * h1 + x * h2
    sem = iter(range(sems.shape[1]))

    def push(src, dst, device):
        k = next(sem)
        copy = pltpu.make_async_remote_copy(
            src_ref=src, dst_ref=dst, send_sem=sems.at[0, k], recv_sem=sems.at[1, k],
            device_id=device, device_id_type=MESH,
        )
        copy.start()
        return copy

    partner = {"attr": x * 2 + 1 - half}
    columns = [lax.rem(x + d, n_x) for d in range(1, n_x)]
    lines = [lax.rem(rec + d, n_rec) for d in range(1, n_rec)]
    copies = [push(buf.at[pl.ds(first + (1 - half) * h1, h1)], r1, partner)]
    yield
    settle(copies)
    for b in range(h1):
        s1[b] = (buf[first + half * h1 + b].astype(F32) + r1[b].astype(F32)).astype(BF16)
    copies = [
        push(s1.at[pl.ds(c * h2, h2)], r2.at[d], {"attr": c * 2 + half}) for d, c in enumerate(columns)
    ]
    yield
    settle(copies)
    for b in range(h2):
        value = s1[x * h2 + b].astype(F32)
        for d in range(n_x - 1):
            value += r2[d, b].astype(F32)
        s2[b] = value.astype(BF16)
    copies = [push(s2.at[:, r], r3.at[d], {"rec": r}) for d, r in enumerate(lines)]
    yield
    settle(copies)
    for b in range(h2):
        value = s2[b, rec].astype(F32)
        for d in range(n_rec - 1):
            value += r3[d, b].astype(F32)
        out[base + b, rec] = value.astype(BF16)
    own = out.at[pl.ds(base, h2), rec]
    copies = [push(own, own, {"rec": r}) for r in lines]
    yield
    settle(copies)
    own = out.at[pl.ds(base, h2)]
    copies = [push(own, own, {"attr": c * 2 + half}) for c in columns]
    yield
    settle(copies)
    own = out.at[pl.ds(first + half * h1, h1)]
    copies = [push(own, own, partner)]
    yield
    settle(copies)
    yield


COUNTS = (8, 4, 4)


def layer_kernel(
    size_a, size_s, length, few,
    cells_h, cot_h, qkva_h, outa_h, qkvs_h, outs_h, up_h, down_h, split_h, place_h,
    o_got, totals,
    cells, cot, qkva, outa, qkvs, outs, up, down, split, places, in_sems,
    flat, c_send, c_got, g_send, g_got, f_send, f_got, b_send, b_got, o_send,
    x_a, mixed_a, qkv_a, p_a, x_s, g_s, qkv_s, p_s, acc, dm_s, dn_s, bias, grads,
    c_sems, g_sems, f_sems, b_sems, o_sems, *sums,
):
    tokens = flat.shape[0]
    n_a, n_s = tokens // size_a, tokens // size_s
    loads = {}
    pairs = (
        (cells_h, cells), (place_h, places), (cot_h, cot), (qkva_h, qkva), (outa_h, outa),
        (split_h, split), (qkvs_h, qkvs), (outs_h, outs), (up_h, up), (down_h, down),
    )
    for k, (src, dst) in enumerate(pairs):
        loads[k] = pltpu.make_async_copy(src, dst, in_sems.at[k])
        loads[k].start()
    barrier = pltpu.get_barrier_semaphore()
    peers = peers_of(("rec", "attr"))
    for r, a in peers:
        pl.semaphore_signal(barrier, inc=1, device_id={"rec": r, "attr": a}, device_id_type=MESH)

    def at(k):
        return places.at[k:k + 1]

    loads[0].wait()
    loads[1].wait()
    pack(c_send, moved(at(0), rows_of(cells, flat)), few)
    pl.semaphore_wait(barrier, len(peers))
    c_copies = start_swap(("attr",), c_send, c_got, c_sems)
    loads[2].wait()
    pack(g_send, moved(at(1), rows_of(cot, flat)), few)
    g_copies = start_swap(("rec",), g_send, g_got, g_sems)
    for k in range(3, len(pairs)):
        loads[k].wait()
    settle(c_copies)
    x_a[...] = unpack(c_got, flat, few)
    _, mixed, first = attend(x_a, qkva, outa[...], qkv_a, p_a, acc, n_a, size_a, None)
    mixed_a[...] = mixed
    pack(f_send, moved(at(2), first), few)
    f_copies = start_swap(("rec", "attr"), f_send, f_got, f_sems)

    row = lax.broadcasted_iota(jnp.int32, (size_s, size_s), 0)
    column = lax.broadcasted_iota(jnp.int32, (size_s, size_s), 1)
    same = None
    for s in range(size_s // length):
        low, high = s * length, (s + 1) * length
        inside = (row >= low) & (row < high) & (column >= low) & (column < high)
        same = inside if same is None else same | inside
    tiled = jnp.concatenate([split[...].astype(F32)] * (size_s // length), axis=1)
    bias[...] = jnp.where(same, tiled, 0.0).T
    settle(g_copies)
    g_s[...] = moved(at(4), unpack(g_got, flat, few)).astype(BF16)
    settle(f_copies)
    x_s[...] = moved(at(3), unpack(f_got, flat, few)).astype(BF16)
    _, mixed, second = attend(x_s, qkvs, outs[...], qkv_s, p_s, acc, n_s, size_s, bias)
    hat, scale = norm(second.astype(F32))
    normed = hat.astype(BF16)
    g = g_s[...]
    for c in range(up.shape[1] // E):
        w_up = up[:, c * E:(c + 1) * E]
        pre = dot(normed, w_up)
        cdf = 0.5 * (1.0 + lax.erf(pre * (1.0 / math.sqrt(2.0))))
        hidden = (pre * cdf).astype(BF16)
        slope = cdf + pre * (jnp.exp(pre * pre * -0.5) * (1.0 / math.sqrt(2.0 * math.pi)))
        dh = dot(g, down[:, c * E:(c + 1) * E]).astype(BF16).astype(F32)
        dpre = (dh * slope).astype(BF16)
        put(grads, c, dot(normed, dpre, TN))
        put(grads, 4 + c, dot(g, hidden, TN))
        part = dot(dpre, w_up, NT)
        if c == 0:
            dn_s[...] = part
        else:
            dn_s[...] += part
    starts = (0, COUNTS[0], COUNTS[0] + COUNTS[1])
    ffn, samp, attr = (
        total_steps(grads, totals, starts[k], COUNTS[k], *sums[6 * k:6 * k + 6]) for k in range(3)
    )
    next(ffn)
    dn = dn_s[...].astype(BF16).astype(F32)
    g = (g.astype(F32) + norm_back(hat, scale, dn)).astype(BF16)

    def go(*groups):
        def step():
            for group in groups:
                next(group)
        return step

    back = attend_back(
        x_s[...], g, mixed, qkvs, outs[...], qkv_s, p_s, acc, dm_s, grads, starts[1], n_s, size_s,
        (go(ffn), go(), go(ffn)),
    )
    pack(b_send, moved(at(5), back), few)
    b_copies = start_swap(("rec", "attr"), b_send, b_got, b_sems)
    next(samp)
    settle(b_copies)
    go(samp, ffn)()
    g = moved(at(6), unpack(b_got, flat, few)).astype(BF16)
    back = attend_back(
        x_a[...], g, mixed_a[...], qkva, outa[...], qkv_a, p_a, acc, dm_s, grads, starts[2], n_a, size_a,
        (go(ffn), go(samp), go(ffn)),
    )
    next(attr)
    pack(o_send, back.astype(F32), few)
    o_copies = start_swap(("attr",), o_send, o_got, o_sems)
    for steps in (samp, attr, ffn, samp, attr, samp, attr, samp, attr, attr, attr):
        next(steps)
    settle(o_copies)


def finish_kernel(
    factor, few, tokens_h, places_h, total_h, cells, qa, oa, qs, os, gu, gd,
    tokens, places, total, sems, flat, out_flat, tmp,
):
    loads = [
        pltpu.make_async_copy(src, dst, sems.at[k])
        for k, (src, dst) in enumerate(((tokens_h, tokens), (places_h, places), (total_h, total)))
    ]
    for load in loads:
        load.start()
    rows = cells.shape[0]
    loads[0].wait()
    loads[1].wait()
    out_flat[...] = moved(places.at[7:8], unpack(tokens, flat, few))
    for a in range(0, cells.shape[1] // E, 2):
        pair = [out_flat[(a + k) * rows:(a + k + 1) * rows] for k in range(2)]
        cells[:, a * E:(a + 2) * E] = jnp.concatenate(pair, axis=1).astype(BF16)
    loads[2].wait()

    def block(b):
        part = total.shape[2]
        for r in range(total.shape[1]):
            tmp[b, r * part:(r + 1) * part] = total[b, r].astype(F32) * factor
        side = tmp[b]
        return jnp.concatenate([side[:, :E], side[:, E:]], axis=0)

    gu[...] = jnp.concatenate([block(c) for c in range(4)], axis=1)
    gd[...] = jnp.concatenate([block(4 + c) for c in range(4)], axis=1)
    for ref, start in ((qs, 8), (qa, 12)):
        ref[...] = jnp.concatenate([block(start + t) for t in range(3)], axis=1)
    os[...] = block(11)
    oa[...] = block(15)


def local(
    cells, cotangent, qkv_attr, out_attr, qkv_samp, out_samp, up_weight, down_weight, train_split
):
    n_rec, n_attr = lax.axis_size("rec"), lax.axis_size("attr")
    rows, cols = cells.shape[0], cells.shape[1] // E
    tokens = rows * cols
    width = cols * n_attr
    length = rows * n_rec
    few = rows // n_attr
    thin = cols // n_rec
    size = length * max(1, min(256 // length, thin))
    places = jnp.asarray(np.stack([
        place((cols, n_attr, few), (2, 1, 0)),
        place((n_rec, thin, n_attr, few), (3, 0, 1, 2)),
        place((few, n_attr, n_rec, thin), (0, 2, 1, 3)),
        place((few, n_rec, n_attr, thin), (3, 1, 2, 0)),
        place((few, n_rec, thin, n_attr), (2, 1, 3, 0)),
        place((thin, n_rec, n_attr, few), (3, 1, 2, 0)),
        place((few, n_rec, n_attr, thin), (0, 2, 1, 3)),
        place((few, n_attr, cols), (2, 1, 0)),
    ]))
    split = train_split[None, :]
    all_devices = n_rec * n_attr
    part = E // 2 // n_rec
    n_x = n_attr // 2

    def shape(*dims, dtype=BF16):
        return jax.ShapeDtypeStruct(dims, dtype)

    def vmem(*dims, dtype=BF16):
        return pltpu.VMEM(dims, dtype)

    args = (
        cells, cotangent, qkv_attr, out_attr, qkv_samp, out_samp, up_weight, down_weight.T, split, places
    )
    c_buf = vmem(n_attr, cols, few * E)
    g_buf = vmem(n_rec, thin * n_attr, few * E)
    f_buf = vmem(all_devices, thin, few * E)
    table = vmem(tokens, E)
    sums = []
    for count in COUNTS:
        h1 = count // 2
        h2 = h1 // n_x
        sums += [
            vmem(h1, n_rec, part, 2 * E), vmem(max(1, n_x - 1), h2, n_rec, part, 2 * E),
            vmem(max(1, n_rec - 1), h2, part, 2 * E), vmem(h1, n_rec, part, 2 * E),
            vmem(h2, n_rec, part, 2 * E),
            pltpu.SemaphoreType.DMA((2, 2 * (n_rec + n_x - 1))),
        ]
    o_got, totals = pl.pallas_call(
        functools.partial(layer_kernel, width, size, length, few),
        out_shape=[shape(n_attr, cols, few * E), shape(BLOCKS, n_rec, part, 2 * E)],
        in_specs=[HBM] * len(args),
        out_specs=[VMEM] * 2,
        scratch_shapes=[pltpu.VMEM(a.shape, a.dtype) for a in args]
        + [
            pltpu.SemaphoreType.DMA((len(args),)),
            vmem(tokens, E, dtype=F32), c_buf, c_buf, g_buf, g_buf, f_buf, f_buf, f_buf, f_buf, c_buf,
            table, table, vmem(3, E, tokens), vmem(tokens // width, HEADS, width, width, dtype=F32),
            table, table, vmem(3, E, tokens), vmem(tokens // size, HEADS, size, size, dtype=F32),
            vmem(3, E, tokens, dtype=F32), vmem(E, tokens), vmem(tokens, E, dtype=F32),
            vmem(size, size, dtype=F32), vmem(BLOCKS, n_rec, part, 2 * E),
        ]
        + [
            pltpu.SemaphoreType.DMA((2, n))
            for n in (n_attr, n_rec, all_devices, all_devices, n_attr)
        ]
        + sums,
        compiler_params=pltpu.CompilerParams(
            collective_id=0, has_side_effects=True, vmem_limit_bytes=67043328
        ),
    )(*args)
    outs = [
        shape(rows, cols * E), shape(E, 3 * E, dtype=F32), shape(E, E, dtype=F32),
        shape(E, 3 * E, dtype=F32), shape(E, E, dtype=F32),
        shape(E, 4 * E, dtype=F32), shape(E, 4 * E, dtype=F32),
    ]
    last = (o_got, places, totals)
    out = pl.pallas_call(
        functools.partial(finish_kernel, 1.0 / math.sqrt(length * width), few),
        out_shape=outs,
        in_specs=[ANY] * 3,
        out_specs=[VMEM] * len(outs),
        scratch_shapes=[pltpu.VMEM(a.shape, a.dtype) for a in last]
        + [
            pltpu.SemaphoreType.DMA((3,)), vmem(tokens, E, dtype=F32), vmem(tokens, E, dtype=F32),
            vmem(BLOCKS, E // 2, 2 * E, dtype=F32),
        ],
        compiler_params=pltpu.CompilerParams(vmem_limit_bytes=67043328),
    )(*last)
    return (*out[:6], out[6].T)


def solution(mesh):
    both = P(("groups", "rec"), "attr")
    in_specs = (both, both, P(), P(), P(), P(), P(), P(), P("groups"))
    out_specs = (both,) + (P("groups", None),) * 6
    return jax.shard_map(local, mesh=mesh, in_specs=in_specs, out_specs=out_specs, check_vma=False)
```
